128 devices in a mesh: grp: 2 (over core), row: 8 (over x_lo, y), col: 8 (over z, x_hi).
Axes of the slice: x: 4 (x_hi: 2, x_lo: 2; x = x_hi * 2 + x_lo), y: 4, z: 4, core: 2. Of those that a mesh axis runs over, the one named last changes fastest.
Arguments:
- conserved: float32 [5, 512, 4096], P(None, 'row', 'col'), may hold values from -1 to 5.5, as said below
- displacement: float32 [2, 512, 4096], P(None, ('row', 'col')), may hold values from -0.3 to 0.3
Outputs:
- group_fields: float32 [2, 5, 512, 4096], P('grp', None, 'row', 'col')
The draws below stay inside these ranges and needn't reach their ends.
Inputs may be any that keep to these rules, and one draw needn't show every extreme that they name: `conserved`: per cell: density and pressure (0.4 times the energy minus the kinetic energy) lie between 1 and 2, both speeds between -0.5 and 0.5, the tracer fraction between 0 and 1.
All inputs are finite; a program needn't handle non-finite values.
Results may differ from the reference program's by a relative error of at most 0.0003.
Values sent between devices are 32-bit elements; how exact they have to be, the bound alone decides.
No kernel may reach another device: no remote copies, remote signals or barrier semaphores. Data moves between devices by JAX's collectives and lax.ppermute only.
A program may use at most 64 MiB of HBM per device.

```python
import jax
import jax.numpy as jnp
from jax import lax

STEPS = 2
SWEEPS = 4
NR = 512
NC = 4096


def draw_conserved(key, part):
    subkeys = jax.random.split(key, 5)
    grid_shape = (NR, NC)
    density = jax.random.uniform(subkeys[0], grid_shape, jnp.float32, 1.0, 2.0)
    speed_x = jax.random.uniform(subkeys[1], grid_shape, jnp.float32, -0.5, 0.5)
    speed_y = jax.random.uniform(subkeys[2], grid_shape, jnp.float32, -0.5, 0.5)
    pressure = jax.random.uniform(subkeys[3], grid_shape, jnp.float32, 1.0, 2.0)
    tracer = jax.random.uniform(subkeys[4], grid_shape, jnp.float32)
    energy = pressure / 0.4 + 0.5 * density * (speed_x * speed_x + speed_y * speed_y)
    return jnp.stack([density, density * speed_x, density * speed_y, energy, density * tracer]).astype(jnp.float32)


def level_of(stream_key, shape, pieces, smallest, top_value):
    factor_of, own = 1.0, jax.random.fold_in(stream_key, 6)
    for axis_at, parts in pieces:
        steps = jnp.exp(jax.random.uniform(jax.random.fold_in(own, axis_at), (parts,), jnp.float32, smallest / len(pieces), top_value / len(pieces)))
        factor_of = factor_of * jnp.repeat(steps, shape[axis_at] // parts).reshape([-1 if axis == axis_at else 1 for axis in range(len(shape))])
    return factor_of


def setup_inputs(seed: int = 0) -> dict:
    seeds = jax.random.split(jax.random.key(seed), 3)
    return {
        "conserved": draw_conserved(jax.random.fold_in(seeds[2], 71), 0),
        "displacement": jnp.clip(jax.random.uniform(seeds[1], (2, NR, NC), jnp.float32, -0.3, 0.3) * level_of(seeds[1], (2, NR, NC), ((1, 64),), -0.4, 0.0), -0.3, 0.3),
    }


HEAT_RATIO = 1.4
TIME_STEP = 0.08
GRADIENT_GAIN = 8.0
MONITOR_GAIN = 0.2
RELAXATION = 0.5

def minmod(lower_diff, upper_diff):
    smaller = jnp.where(jnp.abs(lower_diff) < jnp.abs(upper_diff), lower_diff, upper_diff)
    return jnp.where(lower_diff * upper_diff > 0.0, smaller, 0.0)

def primitives(fields):
    density = fields[0]
    speed_x = fields[1] / density
    speed_y = fields[2] / density
    pressure = (HEAT_RATIO - 1.0) * (fields[3] - 0.5 * (fields[1] * speed_x + fields[2] * speed_y))
    tracer = fields[4] / density
    return jnp.stack([density, speed_x, speed_y, pressure, tracer])

def normal_flux(states, normal_x, normal_y):
    density, speed_x, speed_y, pressure, tracer = (states[0], states[1], states[2], states[3], states[4])
    normal_speed = speed_x * normal_x + speed_y * normal_y
    energy = pressure / (HEAT_RATIO - 1.0) + 0.5 * density * (speed_x * speed_x + speed_y * speed_y)
    conserved = jnp.stack([density, density * speed_x, density * speed_y, energy, density * tracer])
    flux_terms = jnp.stack([density * normal_speed, density * speed_x * normal_speed + pressure * normal_x, density * speed_y * normal_speed + pressure * normal_y, (energy + pressure) * normal_speed, density * tracer * normal_speed])
    wave_speed = jnp.abs(normal_speed) + jnp.sqrt(HEAT_RATIO * pressure / density) * jnp.sqrt(normal_x * normal_x + normal_y * normal_y)
    return (conserved, flux_terms, wave_speed)

def rusanov(left_state, right_state, normal_x, normal_y):
    cons_left, flux_left, wave_left = normal_flux(left_state, normal_x, normal_y)
    cons_right, flux_right, wave_right = normal_flux(right_state, normal_x, normal_y)
    wave_speed = jnp.maximum(wave_left, wave_right)
    return 0.5 * (flux_left + flux_right) - 0.5 * wave_speed * (cons_right - cons_left)

def face_states(primitive, along_axis):
    extent = primitive.shape[along_axis]
    differences = lax.slice_in_dim(primitive, 1, extent, axis=along_axis) - lax.slice_in_dim(primitive, 0, extent - 1, axis=along_axis)
    slopes = minmod(lax.slice_in_dim(differences, 0, extent - 2, axis=along_axis), lax.slice_in_dim(differences, 1, extent - 1, axis=along_axis))
    left_state = lax.slice_in_dim(primitive, 1, extent - 2, axis=along_axis) + 0.5 * lax.slice_in_dim(slopes, 0, extent - 3, axis=along_axis)
    right_state = lax.slice_in_dim(primitive, 2, extent - 1, axis=along_axis) - 0.5 * lax.slice_in_dim(slopes, 1, extent - 2, axis=along_axis)
    return (left_state, right_state)

def advance(extended):
    primitive = primitives(extended[:5])
    shift_x = extended[5]
    shift_y = extended[6]
    slope_x_col = 1.0 + 0.5 * (shift_x[1:-1, 2:] - shift_x[1:-1, :-2])
    slope_x_row = 0.5 * (shift_x[2:, 1:-1] - shift_x[:-2, 1:-1])
    slope_y_col = 0.5 * (shift_y[1:-1, 2:] - shift_y[1:-1, :-2])
    slope_y_row = 1.0 + 0.5 * (shift_y[2:, 1:-1] - shift_y[:-2, 1:-1])
    normal_x = 0.5 * (slope_y_row[1:-1, :-1] + slope_y_row[1:-1, 1:])
    normal_y = -0.5 * (slope_x_row[1:-1, :-1] + slope_x_row[1:-1, 1:])
    left_state, right_state = face_states(primitive[:, 2:-2, :], 2)
    col_flux = rusanov(left_state, right_state, normal_x, normal_y)
    normal_x = -0.5 * (slope_y_col[:-1, 1:-1] + slope_y_col[1:, 1:-1])
    normal_y = 0.5 * (slope_x_col[:-1, 1:-1] + slope_x_col[1:, 1:-1])
    left_state, right_state = face_states(primitive[:, :, 2:-2], 1)
    row_flux = rusanov(left_state, right_state, normal_x, normal_y)
    jacobian = slope_x_col[1:-1, 1:-1] * slope_y_row[1:-1, 1:-1] - slope_x_row[1:-1, 1:-1] * slope_y_col[1:-1, 1:-1]
    change = col_flux[:, :, 1:] - col_flux[:, :, :-1] + (row_flux[:, 1:, :] - row_flux[:, :-1, :])
    return extended[:5, 2:-2, 2:-2] - TIME_STEP / jacobian * change

def monitor(density, pressure):
    density_col = 0.5 * (density[1:-1, 2:] - density[1:-1, :-2])
    density_row = 0.5 * (density[2:, 1:-1] - density[:-2, 1:-1])
    pressure_col = 0.5 * (pressure[1:-1, 2:] - pressure[1:-1, :-2])
    pressure_row = 0.5 * (pressure[2:, 1:-1] - pressure[:-2, 1:-1])
    strength = GRADIENT_GAIN * (density_col * density_col + density_row * density_row + pressure_col * pressure_col + pressure_row * pressure_row)
    return 1.0 + MONITOR_GAIN * strength / (1.0 + strength)

def jacobi(shifts, weight):
    center = weight[1:-1, 1:-1]
    east_face = 0.5 * (center + weight[1:-1, 2:])
    west_face = 0.5 * (center + weight[1:-1, :-2])
    north_face = 0.5 * (center + weight[2:, 1:-1])
    south_face = 0.5 * (center + weight[:-2, 1:-1])
    face_total = east_face + west_face + north_face + south_face
    middle = shifts[:, 1:-1, 1:-1]
    beside_all = east_face * shifts[:, 1:-1, 2:] + west_face * shifts[:, 1:-1, :-2] + north_face * shifts[:, 2:, 1:-1] + south_face * shifts[:, :-2, 1:-1]
    source = jnp.stack([east_face - west_face, north_face - south_face])
    target = (beside_all + source) / face_total
    return middle + RELAXATION * (target - middle)

def wrap_fields(values, margin):
    return jnp.pad(values, ((0, 0), (margin, margin), (margin, margin)), mode='wrap')

def wrap_plane(values, margin):
    return jnp.pad(values, ((margin, margin), (margin, margin)), mode='wrap')

def reference(conserved, displacement):
    current = conserved
    shifts = displacement
    previous = shifts
    weight = jnp.zeros(shifts.shape[1:], jnp.float32)
    for step_index in range(STEPS):
        primitive = primitives(current)
        padded = wrap_fields(jnp.stack([primitive[0], primitive[3]]), 1)
        weight = monitor(padded[0], padded[1])
        start_shifts = shifts
        for sweep_index in range(SWEEPS):
            shifts = jacobi(wrap_fields(shifts, 1), wrap_plane(weight, 1))
        current = advance(wrap_fields(jnp.concatenate([current, start_shifts]), 2))
        previous = start_shifts
    mesh_fields = jnp.stack([shifts[0], shifts[1], (shifts[0] - previous[0]) / TIME_STEP, (shifts[1] - previous[1]) / TIME_STEP, weight])
    return jnp.stack([current, mesh_fields])
```

```python
import jax
import jax.numpy as jnp
from jax import lax
from jax.experimental import pallas as pl
from jax.experimental.pallas import tpu as pltpu
from jax.sharding import PartitionSpec as P

SWEEPS = 4
HEAT_RATIO = 1.4
TIME_STEP = 0.08
GRADIENT_GAIN = 8.0
MONITOR_GAIN = 0.2

BAND = 11
EXT = 8 * BAND
PAD = 12
ROW_HALO = 9
DISP_HALO = 8
EDGE = 128


def next_col(x):
    return pltpu.roll(x, x.shape[1] - 1, 1)


def prev_col(x):
    return pltpu.roll(x, 1, 1)


def next_band(x):
    return pltpu.roll(x, 7, 0)


def prev_band(x):
    return pltpu.roll(x, 1, 0)


def minmod(a, b):
    return jnp.maximum(jnp.minimum(a, b), 0.0) + jnp.minimum(jnp.maximum(a, b), 0.0)


def twice_flux(left, right, nx, ny):
    n2 = HEAT_RATIO * (nx * nx + ny * ny)

    def one(state):
        rho, u, v, p, q = state
        mu, mv, mq = rho * u, rho * v, rho * q
        energy = (1.0 / (HEAT_RATIO - 1.0)) * p + 0.5 * (mu * u + mv * v)
        speed = u * nx + v * ny
        x = p * n2
        wave = jnp.abs(speed) + x * lax.rsqrt(jnp.maximum(x * rho, 1e-30))
        flux = (rho * speed, mu * speed + p * nx, mv * speed + p * ny, (energy + p) * speed, mq * speed)
        return (rho, mu, mv, energy, mq), flux, wave

    cl, fl, sl = one(left)
    cr, fr, sr = one(right)
    s = jnp.maximum(sl, sr)
    return [fl[k] + fr[k] - s * (cr[k] - cl[k]) for k in range(5)]


def each_row(body, unroll=1):
    lax.fori_loop(0, BAND, lambda t, carry: (body(t), carry)[1], 0, unroll=unroll)


def to_primitives(load, prim):
    for t in range(BAND):
        rho, mx, my, en, tr = load(t)
        inv = 1.0 / rho
        u, v = mx * inv, my * inv
        p = (HEAT_RATIO - 1.0) * (en - 0.5 * (mx * u + my * v))
        for k, x in enumerate((rho, u, v, p, tr * inv)):
            prim[k, t + 2] = x
    for k in range(5):
        prim[k, 0] = prev_band(prim[k, BAND])
        prim[k, 1] = prev_band(prim[k, BAND + 1])
        prim[k, BAND + 2] = next_band(prim[k, 2])
        prim[k, BAND + 3] = next_band(prim[k, 3])


def wrap_rows(ref, *lead):
    ref[(*lead, 0)] = prev_band(ref[(*lead, BAND)])
    ref[(*lead, BAND + 1)] = next_band(ref[(*lead, 1)])


def to_weight(prim, weight):
    def body(t):
        g = 0.0
        for k in (0, 3):
            x = prim[k, t + 2]
            a = next_col(x) - prev_col(x)
            b = prim[k, t + 3] - prim[k, t + 1]
            g = g + (a * a + b * b)
        g = (0.25 * GRADIENT_GAIN) * g
        weight[t + 1] = (1.0 + MONITOR_GAIN) - MONITOR_GAIN / (1.0 + g)

    each_row(body)
    wrap_rows(weight)


def to_coefs(weight, coef):
    def body(t):
        c = weight[t + 1]
        e = c + next_col(c)
        w = c + prev_col(c)
        n = c + weight[t + 2]
        s = c + weight[t]
        k = 0.5 / ((e + w) + (n + s))
        coef[0, t] = e * k
        coef[1, t] = w * k
        coef[2, t] = n * k
        coef[3, t] = s * k

    each_row(body)


def sweep(src, dst, coef):
    def body(t):
        he, hw, hn, hs = coef[0, t], coef[1, t], coef[2, t], coef[3, t]
        for k in range(2):
            x = src[k, t + 1]
            source = he - hw if k == 0 else hn - hs
            beside = he * next_col(x) + hw * prev_col(x) + (hn * src[k, t + 2] + hs * src[k, t])
            dst[k, t + 1] = (0.5 * x + source) + beside

    each_row(body)
    for k in range(2):
        wrap_rows(dst, k)


def to_metrics(disp, face, slope):
    def body(t):
        dx, dy = disp[0, t + 1], disp[1, t + 1]
        xc = 1.0 + 0.5 * (next_col(dx) - prev_col(dx))
        yc = 0.5 * (next_col(dy) - prev_col(dy))
        xr = 0.5 * (disp[0, t + 2] - disp[0, t])
        yr = 1.0 + 0.5 * (disp[1, t + 2] - disp[1, t])
        face[0, t] = 0.5 * (yr + next_col(yr))
        face[1, t] = -0.5 * (xr + next_col(xr))
        face[2, t] = (0.5 * TIME_STEP) / (xc * yr - xr * yc)
        slope[0, t] = xc
        slope[1, t] = yc

    each_row(body)
    for k in range(2):
        slope[k, BAND] = next_band(slope[k, 0])


def to_changes(prim, half, face, slope, colch, rowfl):
    def slopes(t):
        for k in range(5):
            x = prim[k, t + 2]
            half[k, t] = minmod(0.5 * (x - prim[k, t + 1]), 0.5 * (prim[k, t + 3] - x))

    each_row(slopes)
    for k in range(5):
        half[k, BAND] = next_band(half[k, 0])

    def body(t):
        left, right = [], []
        for k in range(5):
            x = prim[k, t + 2]
            d = 0.5 * (next_col(x) - x)
            h = minmod(d, prev_col(d))
            left.append(x + h)
            right.append(next_col(x - h))
        flux = twice_flux(left, right, face[0, t], face[1, t])
        for k in range(5):
            colch[k, t] = flux[k] - prev_col(flux[k])

    each_row(body)

    def rbody(t):
        nx = -0.5 * (slope[1, t] + slope[1, t + 1])
        ny = 0.5 * (slope[0, t] + slope[0, t + 1])
        left = [prim[k, t + 2] + half[k, t] for k in range(5)]
        right = [prim[k, t + 3] - half[k, t + 1] for k in range(5)]
        flux = twice_flux(left, right, nx, ny)
        for k in range(5):
            rowfl[k, t + 1] = flux[k]

    each_row(rbody)
    for k in range(5):
        rowfl[k, 0] = prev_band(rowfl[k, BAND])


def core(u_ref, tile_ref, top_ref, bot_ref, dblk_ref, dtop_ref, dbot_ref, out_ref,
         ext, prim, half, face, slope, colch, rowfl, weight, coef, da, db, cons, flat):
    rows, cols = u_ref.shape[1], u_ref.shape[2]
    wide = cols + EDGE
    tiles = wide // EDGE

    def place(k, row, value):
        for j in range(value.shape[1] // EDGE):
            ext[k, j, row:row + value.shape[0], :] = value[:, EDGE * j:EDGE * (j + 1)]

    for k in range(5):
        place(k, PAD, u_ref[k])
        ext[k, tiles - 1, PAD:PAD + rows, :] = tile_ref[k]
        place(k, PAD - ROW_HALO, top_ref[k, 16 - ROW_HALO:16])
        place(k, PAD + rows, bot_ref[k, :ROW_HALO])
    for k in range(2):
        for c in range(dblk_ref.shape[0]):
            place(5 + k, PAD + 8 * c, dblk_ref[c, k])
        place(5 + k, PAD - DISP_HALO, dtop_ref[k])
        place(5 + k, PAD + rows, dbot_ref[k])

    def band(k, t):
        return jnp.concatenate([ext[k, j, pl.ds(t, 8, stride=BAND), :] for j in range(tiles)], 1)

    to_primitives(lambda t: [band(k, t) for k in range(5)], prim)
    for k in range(2):
        for t in range(BAND):
            da[k, t + 1] = band(5 + k, t)
        wrap_rows(da, k)
    to_metrics(da, face, slope)
    to_weight(prim, weight)
    to_coefs(weight, coef)
    src, dst = da, db
    for _ in range(SWEEPS):
        sweep(src, dst, coef)
        src, dst = dst, src
    to_changes(prim, half, face, slope, colch, rowfl)
    for t in range(BAND):
        scale = face[2, t]
        for k in range(5):
            cons[k, t] = band(k, t) - scale * (colch[k, t] + (rowfl[k, t + 1] - rowfl[k, t]))
    to_primitives(lambda t: [cons[k, t] for k in range(5)], prim)

    def put(k, t, x):
        for j in range(tiles - 1):
            flat[k, j, pl.ds(t, 8, stride=BAND), :] = x[:, EDGE * j:EDGE * (j + 1)]

    group = lax.axis_index("grp")

    @pl.when(group == 0)
    def _():
        to_metrics(da, face, slope)
        to_changes(prim, half, face, slope, colch, rowfl)
        for t in range(BAND):
            scale = face[2, t]
            for k in range(5):
                put(k, t, cons[k, t] - scale * (colch[k, t] + (rowfl[k, t + 1] - rowfl[k, t])))

    @pl.when(group == 1)
    def _():
        for t in range(BAND):
            for k in range(2):
                cons[k, t] = da[k, t + 1]
        to_weight(prim, weight)
        to_coefs(weight, coef)
        src, dst = da, db
        for _ in range(SWEEPS):
            sweep(src, dst, coef)
            src, dst = dst, src
        for t in range(BAND):
            for k in range(2):
                put(k, t, da[k, t + 1])
                put(k + 2, t, (da[k, t + 1] - cons[k, t]) * (1.0 / TIME_STEP))
            put(4, t, weight[t + 1])

    for k in range(5):
        for j in range(tiles - 1):
            out_ref[0, k, :, EDGE * j:EDGE * (j + 1)] = flat[k, j, PAD:PAD + rows, :]


def compute(u, tile, top, bot, dblk, dtop, dbot):
    rows, cols = u.shape[1], u.shape[2]
    wide = cols + EDGE
    vec = lambda *lead: pltpu.VMEM((*lead, 8, wide), jnp.float32)
    return pl.pallas_call(
        core,
        out_shape=jax.ShapeDtypeStruct((1, 5, rows, cols), jnp.float32),
        in_specs=[pl.BlockSpec(memory_space=pltpu.VMEM)] * 7,
        out_specs=pl.BlockSpec(memory_space=pltpu.VMEM),
        scratch_shapes=[
            pltpu.VMEM((7, wide // EDGE, EXT, EDGE), jnp.float32),
            vec(5, BAND + 4), vec(5, BAND + 1), vec(3, BAND), vec(2, BAND + 1),
            vec(5, BAND), vec(5, BAND + 1), vec(BAND + 2), vec(4, BAND),
            vec(2, BAND + 2), vec(2, BAND + 2), vec(5, BAND),
            pltpu.VMEM((5, cols // EDGE, EXT, EDGE), jnp.float32),
        ],
        name="euler_mesh",
    )(u, tile, top, bot, dblk, dtop, dbot)


def shift(x, axis, step):
    count = lax.axis_size(axis)
    return lax.ppermute(x, axis, [(i, (i + step) % count) for i in range(count)])


def on_device(conserved, displacement):
    cols = conserved.shape[2]
    parts = lax.axis_size("col")
    lane = lax.broadcasted_iota(jnp.int32, (1, 1, EDGE), 2)
    from_left = shift(conserved[:, :, cols - EDGE:], "col", 1)
    from_right = shift(conserved[:, :, :EDGE], "col", -1)
    pieces = displacement.reshape(2, displacement.shape[1], parts, cols).transpose(2, 0, 1, 3)
    right = jnp.roll(pieces, -1, 0)[..., :EDGE]
    left = jnp.roll(pieces, 1, 0)[..., cols - EDGE:]
    pieces = jnp.concatenate([pieces, jnp.where(lane < EDGE // 2, right, left)], -1)
    dblk = lax.all_to_all(pieces, "col", 0, 0, tiled=True)
    tile = jnp.where(lane < EDGE // 2, from_right, from_left)
    bottom = jnp.concatenate([conserved[:, -16:], tile[:, -16:]], 2)
    upper = jnp.concatenate([conserved[:, :16], tile[:, :16]], 2)
    top = shift(bottom, "row", 1)
    dtop = shift(dblk[-1], "row", 1)
    bot = shift(upper, "row", -1)
    dbot = shift(dblk[0], "row", -1)
    return compute(conserved, tile, top, bot, dblk, dtop, dbot)


def solution(mesh):
    placed = (P(None, "row", "col"), P(None, ("row", "col"), None))
    return jax.shard_map(
        on_device,
        mesh=mesh,
        in_specs=placed,
        out_specs=P("grp", None, "row", "col"),
        check_vma=False,
    )
```

```python
import jax
import jax.numpy as jnp
from jax import lax
from jax.experimental import pallas as pl
from jax.experimental.pallas import tpu as pltpu
from jax.sharding import PartitionSpec as P

SWEEPS = 4
HEAT_RATIO = 1.4
TIME_STEP = 0.08
GRADIENT_GAIN = 8.0
MONITOR_GAIN = 0.2

BAND = 10
EXT = 8 * BAND
PAD = 8
EDGE = 128
SLOT = 16


def next_col(x):
    return pltpu.roll(x, x.shape[1] - 1, 1)


def prev_col(x):
    return pltpu.roll(x, 1, 1)


def next_band(x):
    return pltpu.roll(x, 7, 0)


def prev_band(x):
    return pltpu.roll(x, 1, 0)


def minmod(a, b):
    return jnp.maximum(jnp.minimum(a, b), 0.0) + jnp.minimum(jnp.maximum(a, b), 0.0)


def twice_flux(left, right, nx, ny):
    n2 = HEAT_RATIO * (nx * nx + ny * ny)

    def one(state):
        rho, u, v, p, q = state
        mu, mv, mq = rho * u, rho * v, rho * q
        energy = (1.0 / (HEAT_RATIO - 1.0)) * p + 0.5 * (mu * u + mv * v)
        speed = u * nx + v * ny
        x = p * n2
        wave = jnp.abs(speed) + x * lax.rsqrt(jnp.maximum(x * rho, 1e-30))
        flux = (rho * speed, mu * speed + p * nx, mv * speed + p * ny, (energy + p) * speed, mq * speed)
        return (rho, mu, mv, energy, mq), flux, wave

    cl, fl, sl = one(left)
    cr, fr, sr = one(right)
    s = jnp.maximum(sl, sr)
    return [fl[k] + fr[k] - s * (cr[k] - cl[k]) for k in range(5)]


def each_row(body, unroll):
    def steps(i, carry):
        for n in range(unroll):
            body(i * unroll + n)
        return carry

    if unroll >= BAND:
        for t in range(BAND):
            body(t)
    else:
        lax.fori_loop(0, BAND // unroll, steps, 0)


def primitives_of(rho, mx, my, en, tr):
    inv = 1.0 / rho
    u, v = mx * inv, my * inv
    p = (HEAT_RATIO - 1.0) * (en - 0.5 * (mx * u + my * v))
    return rho, u, v, p, tr * inv


def wrap_prim(prim):
    for k in range(5):
        prim[k, 0] = prev_band(prim[k, BAND])
        prim[k, 1] = prev_band(prim[k, BAND + 1])
        prim[k, BAND + 2] = next_band(prim[k, 2])
        prim[k, BAND + 3] = next_band(prim[k, 3])


def wrap_rows(ref, *lead):
    ref[(*lead, 0)] = prev_band(ref[(*lead, BAND)])
    ref[(*lead, BAND + 1)] = next_band(ref[(*lead, 1)])


def to_weight(prim, weight):
    def body(t):
        g = 0.0
        for k in (0, 3):
            x = prim[k, t + 2]
            a = next_col(x) - prev_col(x)
            b = prim[k, t + 3] - prim[k, t + 1]
            g = g + (a * a + b * b)
        g = (0.25 * GRADIENT_GAIN) * g
        weight[t + 1] = (1.0 + MONITOR_GAIN) - MONITOR_GAIN / (1.0 + g)

    each_row(body, U_WEIGHT)
    wrap_rows(weight)


def to_coefs(weight, coef):
    def body(t):
        c = weight[t + 1]
        e = c + next_col(c)
        w = c + prev_col(c)
        n = c + weight[t + 2]
        s = c + weight[t]
        k = 0.5 / ((e + w) + (n + s))
        coef[0, t] = e * k
        coef[1, t] = w * k
        coef[2, t] = n * k
        coef[3, t] = s * k

    each_row(body, U_COEF)


def sweep(src, dst, coef):
    def body(t):
        he, hw, hn, hs = coef[0, t], coef[1, t], coef[2, t], coef[3, t]
        for k in range(2):
            x = src[k, t + 1]
            source = he - hw if k == 0 else hn - hs
            beside = he * next_col(x) + hw * prev_col(x) + (hn * src[k, t + 2] + hs * src[k, t])
            dst[k, t + 1] = (0.5 * x + source) + beside

    each_row(body, U_SWEEP)
    for k in range(2):
        wrap_rows(dst, k)


def to_metrics(disp, face, slope):
    def body(t):
        dx, dy = disp[0, t + 1], disp[1, t + 1]
        xc = 1.0 + 0.5 * (next_col(dx) - prev_col(dx))
        yc = 0.5 * (next_col(dy) - prev_col(dy))
        xr = 0.5 * (disp[0, t + 2] - disp[0, t])
        yr = 1.0 + 0.5 * (disp[1, t + 2] - disp[1, t])
        face[0, t] = 0.5 * (yr + next_col(yr))
        face[1, t] = -0.5 * (xr + next_col(xr))
        face[2, t] = (0.5 * TIME_STEP) / (xc * yr - xr * yc)
        slope[0, t] = xc
        slope[1, t] = yc

    each_row(body, U_METRIC)
    for k in range(2):
        slope[k, BAND] = next_band(slope[k, 0])


def to_fluxes(prim, half, side, face, slope, colfl, rowfl):
    def slopes(t):
        for k in range(5):
            x = prim[k, t + 2]
            half[k, t] = minmod(0.5 * (x - prim[k, t + 1]), 0.5 * (prim[k, t + 3] - x))
            d = 0.5 * (next_col(x) - x)
            h = minmod(d, prev_col(d))
            side[k, t] = x + h
            side[5 + k, t] = next_col(x - h)

    each_row(slopes, U_SLOPE)
    for k in range(5):
        half[k, BAND] = next_band(half[k, 0])
    wide = prim.shape[3]

    def fluxes(t):
        for j in range(wide // EDGE):
            at = slice(EDGE * j, EDGE * (j + 1))
            left = [side[k, t, :, at] for k in range(5)]
            right = [side[5 + k, t, :, at] for k in range(5)]
            flux = twice_flux(left, right, face[0, t, :, at], face[1, t, :, at])
            for k in range(5):
                colfl[k, t, :, at] = flux[k]
            nx = -0.5 * (slope[1, t, :, at] + slope[1, t + 1, :, at])
            ny = 0.5 * (slope[0, t, :, at] + slope[0, t + 1, :, at])
            left = [prim[k, t + 2, :, at] + half[k, t, :, at] for k in range(5)]
            right = [prim[k, t + 3, :, at] - half[k, t + 1, :, at] for k in range(5)]
            flux = twice_flux(left, right, nx, ny)
            for k in range(5):
                rowfl[k, t + 1, :, at] = flux[k]

    each_row(fluxes, U_FLUX)
    for k in range(5):
        rowfl[k, 0] = prev_band(rowfl[k, BAND])


def change(k, t, face, colfl, rowfl):
    c = colfl[k, t]
    return face[2, t] * ((c - prev_col(c)) + (rowfl[k, t + 1] - rowfl[k, t]))


def unpack_edges(left, right, k):
    lane = lax.broadcasted_iota(jnp.int32, left.shape, 1)
    a = pltpu.roll(right, (EDGE - SLOT * k) % EDGE, 1)
    b = pltpu.roll(left, (EDGE - SLOT - SLOT * k) % EDGE, 1)
    return jnp.where(lane < EDGE // 2, a, b)


def core(u_ref, left_ref, right_ref, dblk_ref, top_ref, bot_ref, out_ref,
         ext, prim, half, side, face, slope, colfl, rowfl, weight, coef, da, db, cons, flat):
    rows, cols = u_ref.shape[1], u_ref.shape[2]
    tiles = cols // EDGE + 1

    def place(k, row, value):
        for j in range(value.shape[1] // EDGE):
            ext[k, j, row:row + value.shape[0], :] = value[:, EDGE * j:EDGE * (j + 1)]

    left, right = left_ref[...], right_ref[...]
    for k in range(5):
        place(k, PAD, u_ref[k])
        ext[k, tiles - 1, PAD:PAD + rows, :] = unpack_edges(left, right, k)
    for k in range(2):
        for c in range(dblk_ref.shape[0]):
            place(5 + k, PAD + 8 * c, dblk_ref[c, k])
    for k in range(7):
        place(k, 0, top_ref[k])
        place(k, PAD + rows, bot_ref[k])

    def band(k, t):
        return jnp.concatenate([ext[k, j, pl.ds(t, 8, stride=BAND), :] for j in range(tiles)], 1)

    for t in range(BAND):
        for k, x in enumerate(primitives_of(*[band(k, t) for k in range(5)])):
            prim[k, t + 2] = x
    wrap_prim(prim)
    sub = lax.broadcasted_iota(jnp.int32, (8, cols + EDGE), 0)
    for ref, at, hit in ((top_ref, 1, 0), (bot_ref, BAND + 2, 7)):
        outer = [jnp.broadcast_to(ref[7, k:k + 1], (8, cols + EDGE)) for k in range(4)]
        extra = primitives_of(*outer, outer[0])
        for k in (0, 3):
            prim[k, at] = jnp.where(sub == hit, extra[k], prim[k, at])
    for k in range(2):
        for t in range(BAND):
            da[k, t + 1] = band(5 + k, t)
        wrap_rows(da, k)
    to_metrics(da, face, slope)
    to_weight(prim, weight)
    to_coefs(weight, coef)
    src, dst = da, db
    for _ in range(SWEEPS):
        sweep(src, dst, coef)
        src, dst = dst, src
    to_fluxes(prim, half, side, face, slope, colfl, rowfl)
    for t in range(BAND):
        new = [band(k, t) - change(k, t, face, colfl, rowfl) for k in range(5)]
        for k in range(5):
            cons[k, t] = new[k]
        for k, x in enumerate(primitives_of(*new)):
            prim[k, t + 2] = x
    wrap_prim(prim)

    def put(k, t, x):
        for j in range(tiles - 1):
            flat[k, j, pl.ds(t, 8, stride=BAND), :] = x[:, EDGE * j:EDGE * (j + 1)]

    group = lax.axis_index("grp")

    @pl.when(group == 0)
    def _():
        to_metrics(da, face, slope)
        to_fluxes(prim, half, side, face, slope, colfl, rowfl)
        for t in range(BAND):
            for k in range(5):
                put(k, t, cons[k, t] - change(k, t, face, colfl, rowfl))

    @pl.when(group == 1)
    def _():
        for t in range(BAND):
            for k in range(2):
                cons[k, t] = da[k, t + 1]
        to_weight(prim, weight)
        to_coefs(weight, coef)
        src, dst = da, db
        for _ in range(SWEEPS):
            sweep(src, dst, coef)
            src, dst = dst, src
        for t in range(BAND):
            for k in range(2):
                put(k, t, da[k, t + 1])
                put(k + 2, t, (da[k, t + 1] - cons[k, t]) * (1.0 / TIME_STEP))
            put(4, t, weight[t + 1])

    for k in range(5):
        for j in range(tiles - 1):
            out_ref[0, k, :, EDGE * j:EDGE * (j + 1)] = flat[k, j, PAD:PAD + rows, :]


U_WEIGHT = U_COEF = U_SWEEP = U_METRIC = U_SLOPE = 5
U_FLUX = 1


def compute(u, left, right, dblk, top, bot):
    rows, cols = u.shape[1], u.shape[2]
    wide = cols + EDGE
    vec = lambda *lead: pltpu.VMEM((*lead, 8, wide), jnp.float32)
    return pl.pallas_call(
        core,
        out_shape=jax.ShapeDtypeStruct((1, 5, rows, cols), jnp.float32),
        in_specs=[pl.BlockSpec(memory_space=pltpu.VMEM)] * 6,
        out_specs=pl.BlockSpec(memory_space=pltpu.VMEM),
        scratch_shapes=[
            pltpu.VMEM((7, wide // EDGE, EXT, EDGE), jnp.float32),
            vec(5, BAND + 4), vec(5, BAND + 1), vec(10, BAND), vec(3, BAND), vec(2, BAND + 1),
            vec(5, BAND), vec(5, BAND + 1), vec(BAND + 2), vec(4, BAND),
            vec(2, BAND + 2), vec(2, BAND + 2), vec(5, BAND),
            pltpu.VMEM((5, cols // EDGE, EXT, EDGE), jnp.float32),
        ],
        name="euler_mesh",
    )(u, left, right, dblk, top, bot)


def pack(first_ref, last_ref, disp_ref, left_ref, right_ref, piece_ref):
    lane = lax.broadcasted_iota(jnp.int32, left_ref.shape, 1)
    left = right = None
    for k in range(5):
        a = pltpu.roll(first_ref[k], SLOT * k, 1) if k else first_ref[k]
        b = pltpu.roll(last_ref[k], (SLOT + SLOT * k) % EDGE, 1)
        left = a if left is None else jnp.where(lane < SLOT * k, left, a)
        right = b if right is None else jnp.where(lane < SLOT * k, right, b)
    left_ref[...] = left
    right_ref[...] = right
    parts = piece_ref.shape[0]
    cols = piece_ref.shape[3] - EDGE
    lane = lax.broadcasted_iota(jnp.int32, (disp_ref.shape[1], EDGE), 1)
    for c in range(parts):
        after = cols * ((c + 1) % parts)
        before = cols * ((c - 1) % parts) + cols - EDGE
        for k in range(2):
            piece_ref[c, k, :, :cols] = disp_ref[k, :, cols * c:cols * (c + 1)]
            piece_ref[c, k, :, cols:] = jnp.where(
                lane < EDGE // 2, disp_ref[k, :, after:after + EDGE], disp_ref[k, :, before:before + EDGE]
            )


def rim(top_ref, bot_ref, left_ref, right_ref, dfirst_ref, dlast_ref, up_ref, down_ref):
    cols = top_ref.shape[2]
    last = bot_ref.shape[1] - 8
    rows = left_ref.shape[0]
    for k in range(5):
        up_ref[k, :, :cols] = top_ref[k, :8]
        up_ref[k, :, cols:] = unpack_edges(left_ref[:8], right_ref[:8], k)
        down_ref[k, :, :cols] = bot_ref[k, last:]
        down_ref[k, :, cols:] = unpack_edges(left_ref[rows - 8:], right_ref[rows - 8:], k)
    for k in range(4):
        up_ref[7, k:k + 1, :cols] = top_ref[k, 8:9]
        up_ref[7, k:k + 1, cols:] = unpack_edges(left_ref[8:16], right_ref[8:16], k)[:1]
        down_ref[7, k:k + 1, :cols] = bot_ref[k, last - 1:last]
        down_ref[7, k:k + 1, cols:] = unpack_edges(left_ref[rows - 16:rows - 8], right_ref[rows - 16:rows - 8], k)[7:]
    for k in range(2):
        up_ref[5 + k] = dfirst_ref[0, k]
        down_ref[5 + k] = dlast_ref[0, k]


def shift(x, axis, step):
    count = lax.axis_size(axis)
    return lax.ppermute(x, axis, [(i, (i + step) % count) for i in range(count)])


def on_device(conserved, displacement):
    rows, cols = conserved.shape[1:]
    parts = lax.axis_size("col")
    slab = displacement.shape[1]
    f32 = jnp.float32
    whole = pl.BlockSpec(memory_space=pltpu.VMEM)
    at = lambda shape, *index: pl.BlockSpec(shape, lambda i: index)
    first, last, pieces = pl.pallas_call(
        pack,
        out_shape=(
            jax.ShapeDtypeStruct((rows, EDGE), f32),
            jax.ShapeDtypeStruct((rows, EDGE), f32),
            jax.ShapeDtypeStruct((parts, 2, slab, cols + EDGE), f32),
        ),
        grid=(1,),
        in_specs=[
            at((5, rows, EDGE), 0, 0, 0),
            at((5, rows, EDGE), 0, 0, cols // EDGE - 1),
            at(displacement.shape, 0, 0, 0),
        ],
        out_specs=(
            at((rows, EDGE), 0, 0),
            at((rows, EDGE), 0, 0),
            at((parts, 2, slab, cols + EDGE), 0, 0, 0, 0),
        ),
        name="pack",
    )(conserved, conserved, displacement)
    dblk = lax.all_to_all(pieces, "col", 0, 0, tiled=True)
    left = shift(last, "col", 1)
    right = shift(first, "col", -1)
    payload = jax.ShapeDtypeStruct((8, 8, cols + EDGE), f32)
    up, down = pl.pallas_call(
        rim,
        out_shape=(payload, payload),
        grid=(1,),
        in_specs=[
            at((5, 16, cols), 0, 0, 0),
            at((5, 16, cols), 0, rows // 16 - 1, 0),
            at((rows, EDGE), 0, 0),
            at((rows, EDGE), 0, 0),
            at((1, 2, slab, cols + EDGE), 0, 0, 0, 0),
            at((1, 2, slab, cols + EDGE), parts - 1, 0, 0, 0),
        ],
        out_specs=(at(payload.shape, 0, 0, 0), at(payload.shape, 0, 0, 0)),
        name="rim",
    )(conserved, conserved, left, right, dblk, dblk)
    top = shift(down, "row", 1)
    bot = shift(up, "row", -1)
    return compute(conserved, left, right, dblk, top, bot)


def solution(mesh):
    placed = (P(None, "row", "col"), P(None, ("row", "col"), None))
    return jax.shard_map(
        on_device,
        mesh=mesh,
        in_specs=placed,
        out_specs=P("grp", None, "row", "col"),
        check_vma=False,
    )
```

```python
import jax
import jax.numpy as jnp
from jax import lax
from jax.experimental import pallas as pl
from jax.experimental.pallas import tpu as pltpu
from jax.sharding import PartitionSpec as P

SWEEPS = 4
HEAT_RATIO = 1.4
TIME_STEP = 0.08
GRADIENT_GAIN = 8.0
MONITOR_GAIN = 0.2

BAND = 10
EXT = 8 * BAND
PAD = 8
EDGE = 128
SLOT = 12
HALF = 32
DTILES = 10


def next_col(x):
    return pltpu.roll(x, x.shape[1] - 1, 1)


def prev_col(x):
    return pltpu.roll(x, 1, 1)


def next_band(x):
    return pltpu.roll(x, 7, 0)


def prev_band(x):
    return pltpu.roll(x, 1, 0)


def minmod(a, b):
    return jnp.maximum(jnp.minimum(a, b), 0.0) + jnp.minimum(jnp.maximum(a, b), 0.0)


def twice_flux(left, right, nx, ny):
    n2 = HEAT_RATIO * (nx * nx + ny * ny)

    def one(state):
        rho, u, v, p, q = state
        mu, mv, mq = rho * u, rho * v, rho * q
        energy = (1.0 / (HEAT_RATIO - 1.0)) * p + 0.5 * (mu * u + mv * v)
        speed = u * nx + v * ny
        x = p * n2
        wave = jnp.abs(speed) + x * lax.rsqrt(jnp.maximum(x * rho, 1e-30))
        flux = (rho * speed, mu * speed + p * nx, mv * speed + p * ny, (energy + p) * speed, mq * speed)
        return (rho, mu, mv, energy, mq), flux, wave

    cl, fl, sl = one(left)
    cr, fr, sr = one(right)
    s = jnp.maximum(sl, sr)
    return [fl[k] + fr[k] - s * (cr[k] - cl[k]) for k in range(5)]


def each_row(body, unroll):
    def steps(i, carry):
        for n in range(unroll):
            body(i * unroll + n)
        return carry

    if unroll >= BAND:
        for t in range(BAND):
            body(t)
    else:
        lax.fori_loop(0, BAND // unroll, steps, 0)


def primitives_of(rho, mx, my, en, tr):
    inv = 1.0 / rho
    u, v = mx * inv, my * inv
    p = (HEAT_RATIO - 1.0) * (en - 0.5 * (mx * u + my * v))
    return rho, u, v, p, tr * inv


def wrap_prim(prim):
    for k in range(5):
        prim[k, 0] = prev_band(prim[k, BAND])
        prim[k, 1] = prev_band(prim[k, BAND + 1])
        prim[k, BAND + 2] = next_band(prim[k, 2])
        prim[k, BAND + 3] = next_band(prim[k, 3])


def wrap_rows(ref, *lead):
    ref[(*lead, 0)] = prev_band(ref[(*lead, BAND)])
    ref[(*lead, BAND + 1)] = next_band(ref[(*lead, 1)])


def to_weight(prim, weight):
    def body(t):
        g = 0.0
        for k in (0, 3):
            x = prim[k, t + 2]
            a = next_col(x) - prev_col(x)
            b = prim[k, t + 3] - prim[k, t + 1]
            g = g + (a * a + b * b)
        g = (0.25 * GRADIENT_GAIN) * g
        weight[t + 1] = (1.0 + MONITOR_GAIN) - MONITOR_GAIN / (1.0 + g)

    each_row(body, U_WEIGHT)
    wrap_rows(weight)


def to_coefs(weight, coef):
    def body(t):
        c = weight[t + 1]
        e = c + next_col(c)
        w = c + prev_col(c)
        n = c + weight[t + 2]
        s = c + weight[t]
        k = 0.5 / ((e + w) + (n + s))
        coef[0, t] = e * k
        coef[1, t] = w * k
        coef[2, t] = n * k
        coef[3, t] = s * k

    each_row(body, U_COEF)


def sweep(src, dst, coef):
    def body(t):
        he, hw, hn, hs = coef[0, t], coef[1, t], coef[2, t], coef[3, t]
        for k in range(2):
            x = src[k, t + 1]
            source = he - hw if k == 0 else hn - hs
            beside = he * next_col(x) + hw * prev_col(x) + (hn * src[k, t + 2] + hs * src[k, t])
            dst[k, t + 1] = (0.5 * x + source) + beside

    each_row(body, U_SWEEP)
    for k in range(2):
        wrap_rows(dst, k)


def to_metrics(disp, face, slope):
    def body(t):
        dx, dy = disp[0, t + 1], disp[1, t + 1]
        xc = 1.0 + 0.5 * (next_col(dx) - prev_col(dx))
        yc = 0.5 * (next_col(dy) - prev_col(dy))
        xr = 0.5 * (disp[0, t + 2] - disp[0, t])
        yr = 1.0 + 0.5 * (disp[1, t + 2] - disp[1, t])
        face[0, t] = 0.5 * (yr + next_col(yr))
        face[1, t] = -0.5 * (xr + next_col(xr))
        face[2, t] = (0.5 * TIME_STEP) / (xc * yr - xr * yc)
        slope[0, t] = xc
        slope[1, t] = yc

    each_row(body, U_METRIC)
    for k in range(2):
        slope[k, BAND] = next_band(slope[k, 0])


def to_fluxes(prim, half, side, face, slope, colfl, rowfl):
    def slopes(t):
        for k in range(5):
            x = prim[k, t + 2]
            half[k, t] = minmod(0.5 * (x - prim[k, t + 1]), 0.5 * (prim[k, t + 3] - x))
            d = 0.5 * (next_col(x) - x)
            h = minmod(d, prev_col(d))
            side[k, t] = x + h
            side[5 + k, t] = next_col(x - h)

    each_row(slopes, U_SLOPE)
    for k in range(5):
        half[k, BAND] = next_band(half[k, 0])
    wide = prim.shape[3]

    def fluxes(t):
        for j in range(wide // EDGE):
            at = slice(EDGE * j, EDGE * (j + 1))
            left = [side[k, t, :, at] for k in range(5)]
            right = [side[5 + k, t, :, at] for k in range(5)]
            flux = twice_flux(left, right, face[0, t, :, at], face[1, t, :, at])
            for k in range(5):
                colfl[k, t, :, at] = flux[k]
            nx = -0.5 * (slope[1, t, :, at] + slope[1, t + 1, :, at])
            ny = 0.5 * (slope[0, t, :, at] + slope[0, t + 1, :, at])
            left = [prim[k, t + 2, :, at] + half[k, t, :, at] for k in range(5)]
            right = [prim[k, t + 3, :, at] - half[k, t + 1, :, at] for k in range(5)]
            flux = twice_flux(left, right, nx, ny)
            for k in range(5):
                rowfl[k, t + 1, :, at] = flux[k]

    each_row(fluxes, U_FLUX)
    for k in range(5):
        rowfl[k, 0] = prev_band(rowfl[k, BAND])


def change(k, t, face, colfl, rowfl):
    c = colfl[k, t]
    return face[2, t] * ((c - prev_col(c)) + (rowfl[k, t + 1] - rowfl[k, t]))


def unpack_edges(left, right, k, half):
    lane = lax.broadcasted_iota(jnp.int32, left.shape, 1)
    start = EDGE // 2 * half + SLOT * k
    a = pltpu.roll(right, (EDGE - start) % EDGE, 1)
    b = pltpu.roll(left, (EDGE - SLOT - start) % EDGE, 1)
    return jnp.where(lane < EDGE // 2, a, b)


def beside(parts):
    c = lax.axis_index("col")
    return lax.rem(c + parts - 1, parts), lax.rem(c + 1, parts)


def core(u_ref, piece_ref, top_ref, bot_ref, out_ref,
         ext, prim, half, side, face, slope, colfl, rowfl, weight, coef, da, db, cons, flat):
    rows, cols = u_ref.shape[1], u_ref.shape[2]
    tiles = cols // EDGE + 1

    def place(k, row, value):
        for j in range(value.shape[1] // EDGE):
            ext[k, j, row:row + value.shape[0], :] = value[:, EDGE * j:EDGE * (j + 1)]

    before, after = beside(piece_ref.shape[0])
    for k in range(5):
        place(k, PAD, u_ref[k])
        for g in range(HALF // 8):
            left, right = piece_ref[before, DTILES + g], piece_ref[after, DTILES + g]
            for h in range(2):
                row = PAD + HALF * h + 8 * g
                ext[k, tiles - 1, row:row + 8, :] = unpack_edges(left, right, k, h)
    for k in range(2):
        for c in range(piece_ref.shape[0]):
            for j in range(tiles):
                ext[5 + k, j, PAD + 8 * c:PAD + 8 * c + 8, :] = piece_ref[c, tiles * k + j]
    for k in range(7):
        place(k, 0, top_ref[k])
        place(k, PAD + rows, bot_ref[k])

    def band(k, t):
        return jnp.concatenate([ext[k, j, pl.ds(t, 8, stride=BAND), :] for j in range(tiles)], 1)

    for t in range(BAND):
        for k, x in enumerate(primitives_of(*[band(k, t) for k in range(5)])):
            prim[k, t + 2] = x
    wrap_prim(prim)
    sub = lax.broadcasted_iota(jnp.int32, (8, cols + EDGE), 0)
    for ref, at, hit in ((top_ref, 1, 0), (bot_ref, BAND + 2, 7)):
        outer = [jnp.broadcast_to(ref[7, k:k + 1], (8, cols + EDGE)) for k in range(4)]
        extra = primitives_of(*outer, outer[0])
        for k in (0, 3):
            prim[k, at] = jnp.where(sub == hit, extra[k], prim[k, at])
    for k in range(2):
        for t in range(BAND):
            da[k, t + 1] = band(5 + k, t)
        wrap_rows(da, k)
    to_metrics(da, face, slope)
    to_weight(prim, weight)
    to_coefs(weight, coef)
    src, dst = da, db
    for _ in range(SWEEPS):
        sweep(src, dst, coef)
        src, dst = dst, src
    to_fluxes(prim, half, side, face, slope, colfl, rowfl)
    for t in range(BAND):
        new = [band(k, t) - change(k, t, face, colfl, rowfl) for k in range(5)]
        for k in range(5):
            cons[k, t] = new[k]
        for k, x in enumerate(primitives_of(*new)):
            prim[k, t + 2] = x
    wrap_prim(prim)

    def put(k, t, x):
        for j in range(tiles - 1):
            flat[k, j, pl.ds(t, 8, stride=BAND), :] = x[:, EDGE * j:EDGE * (j + 1)]

    group = lax.axis_index("grp")

    @pl.when(group == 0)
    def _():
        to_metrics(da, face, slope)
        to_fluxes(prim, half, side, face, slope, colfl, rowfl)
        for t in range(BAND):
            for k in range(5):
                put(k, t, cons[k, t] - change(k, t, face, colfl, rowfl))

    @pl.when(group == 1)
    def _():
        for t in range(BAND):
            for k in range(2):
                cons[k, t] = da[k, t + 1]
        to_weight(prim, weight)
        to_coefs(weight, coef)
        src, dst = da, db
        for _ in range(SWEEPS):
            sweep(src, dst, coef)
            src, dst = dst, src
        for t in range(BAND):
            for k in range(2):
                put(k, t, da[k, t + 1])
                put(k + 2, t, (da[k, t + 1] - cons[k, t]) * (1.0 / TIME_STEP))
            put(4, t, weight[t + 1])

    for k in range(5):
        for j in range(tiles - 1):
            out_ref[0, k, :, EDGE * j:EDGE * (j + 1)] = flat[k, j, PAD:PAD + rows, :]


U_WEIGHT = U_COEF = U_SWEEP = U_METRIC = U_SLOPE = 5
U_FLUX = 1


def near(x):
    return pltpu.with_memory_space_constraint(x, pltpu.VMEM)


def compute(u, pieces, top, bot):
    rows, cols = u.shape[1], u.shape[2]
    wide = cols + EDGE
    vec = lambda *lead: pltpu.VMEM((*lead, 8, wide), jnp.float32)
    return pl.pallas_call(
        core,
        out_shape=jax.ShapeDtypeStruct((1, 5, rows, cols), jnp.float32),
        in_specs=[pl.BlockSpec(memory_space=pltpu.VMEM)] * 4,
        out_specs=pl.BlockSpec(memory_space=pltpu.VMEM),
        scratch_shapes=[
            pltpu.VMEM((7, wide // EDGE, EXT, EDGE), jnp.float32),
            vec(5, BAND + 4), vec(5, BAND + 1), vec(10, BAND), vec(3, BAND), vec(2, BAND + 1),
            vec(5, BAND), vec(5, BAND + 1), vec(BAND + 2), vec(4, BAND),
            vec(2, BAND + 2), vec(2, BAND + 2), vec(5, BAND),
            pltpu.VMEM((5, cols // EDGE, EXT, EDGE), jnp.float32),
        ],
        name="euler_mesh",
    )(u, near(pieces), near(top), near(bot))


def pack(first_ref, last_ref, disp_ref, piece_ref):
    parts = piece_ref.shape[0]
    tiles = DTILES // 2
    cols = EDGE * (tiles - 1)
    before, after = beside(parts)
    lane = lax.broadcasted_iota(jnp.int32, (8, EDGE), 1)
    for g in range(HALF // 8):
        first = last = None
        for half in range(2):
            rows = slice(HALF * half + 8 * g, HALF * half + 8 * g + 8)
            for k in range(5):
                start = EDGE // 2 * half + SLOT * k
                a = pltpu.roll(first_ref[k, rows], start, 1) if start else first_ref[k, rows]
                b = pltpu.roll(last_ref[k, rows], SLOT + start, 1)
                first = a if first is None else jnp.where(lane < start, first, a)
                last = b if last is None else jnp.where(lane < start, last, b)
        piece_ref[before, DTILES + g] = first
        piece_ref[after, DTILES + g] = last
    for c in range(parts):
        right = cols * ((c + 1) % parts)
        left = cols * ((c - 1) % parts) + cols - EDGE
        for k in range(2):
            for j in range(tiles - 1):
                at = cols * c + EDGE * j
                piece_ref[c, tiles * k + j] = disp_ref[k, :, at:at + EDGE]
            piece_ref[c, tiles * k + tiles - 1] = jnp.where(
                lane < EDGE // 2, disp_ref[k, :, right:right + EDGE], disp_ref[k, :, left:left + EDGE]
            )


def rim(top_ref, bot_ref, piece_ref, up_ref, down_ref):
    cols = top_ref.shape[2]
    tiles = cols // EDGE + 1
    end = bot_ref.shape[1] - 8
    parts = piece_ref.shape[0]
    before, after = beside(parts)
    final = DTILES + HALF // 8 - 1
    l0, r0 = piece_ref[before, DTILES], piece_ref[after, DTILES]
    l1, r1 = piece_ref[before, final], piece_ref[after, final]
    for k in range(5):
        up_ref[k, :, :cols] = top_ref[k, :8]
        up_ref[k, :, cols:] = unpack_edges(l0, r0, k, 0)
        down_ref[k, :, :cols] = bot_ref[k, end:]
        down_ref[k, :, cols:] = unpack_edges(l1, r1, k, 1)
    l0, r0 = piece_ref[before, DTILES + 1], piece_ref[after, DTILES + 1]
    l1, r1 = piece_ref[before, final - 1], piece_ref[after, final - 1]
    for k in range(4):
        up_ref[7, k:k + 1, :cols] = top_ref[k, 8:9]
        up_ref[7, k:k + 1, cols:] = unpack_edges(l0, r0, k, 0)[:1]
        down_ref[7, k:k + 1, :cols] = bot_ref[k, end - 1:end]
        down_ref[7, k:k + 1, cols:] = unpack_edges(l1, r1, k, 1)[7:]
    for k in range(2):
        for j in range(tiles):
            up_ref[5 + k, :, EDGE * j:EDGE * (j + 1)] = piece_ref[0, tiles * k + j]
            down_ref[5 + k, :, EDGE * j:EDGE * (j + 1)] = piece_ref[parts - 1, tiles * k + j]


def shift(x, axis, step):
    count = lax.axis_size(axis)
    return lax.ppermute(x, axis, [(i, (i + step) % count) for i in range(count)])


def on_device(conserved, displacement):
    rows, cols = conserved.shape[1:]
    parts = lax.axis_size("col")
    f32 = jnp.float32
    at = lambda shape, *index: pl.BlockSpec(shape, lambda i: index)
    whole = pl.BlockSpec(memory_space=pltpu.VMEM)
    pieces = pl.pallas_call(
        pack,
        out_shape=pltpu.VMEM((parts, DTILES + HALF // 8, 8, EDGE), f32),
        grid=(1,),
        in_specs=[
            at((5, rows, EDGE), 0, 0, 0),
            at((5, rows, EDGE), 0, 0, cols // EDGE - 1),
            at(displacement.shape, 0, 0, 0),
        ],
        out_specs=whole,
        name="pack",
    )(conserved, conserved, displacement)
    pieces = lax.all_to_all(pieces, "col", 0, 0, tiled=True)
    payload = pltpu.VMEM((8, 8, cols + EDGE), f32)
    up, down = pl.pallas_call(
        rim,
        out_shape=(payload, payload),
        grid=(1,),
        in_specs=[
            at((5, 16, cols), 0, 0, 0),
            at((5, 16, cols), 0, rows // 16 - 1, 0),
            whole,
        ],
        out_specs=(whole, whole),
        name="rim",
    )(conserved, conserved, near(pieces))
    top = shift(down, "row", 1)
    bot = shift(up, "row", -1)
    return compute(conserved, pieces, top, bot)


def solution(mesh):
    placed = (P(None, "row", "col"), P(None, ("row", "col"), None))
    return jax.shard_map(
        on_device,
        mesh=mesh,
        in_specs=placed,
        out_specs=P("grp", None, "row", "col"),
        check_vma=False,
    )
```

```python
import jax
import jax.numpy as jnp
from jax import lax
from jax.experimental import pallas as pl
from jax.experimental.pallas import tpu as pltpu
from jax.sharding import PartitionSpec as P

SWEEPS = 4
HEAT_RATIO = 1.4
TIME_STEP = 0.08
GRADIENT_GAIN = 8.0
MONITOR_GAIN = 0.2

BAND = 10
EXT = 8 * BAND
PAD = 8
EDGE = 128
SLOT = 12
HALF = 32
DTILES = 9


def next_col(x):
    return pltpu.roll(x, x.shape[1] - 1, 1)


def prev_col(x):
    return pltpu.roll(x, 1, 1)


def next_band(x):
    return pltpu.roll(x, 7, 0)


def prev_band(x):
    return pltpu.roll(x, 1, 0)


def minmod(a, b):
    return jnp.maximum(jnp.minimum(a, b), 0.0) + jnp.minimum(jnp.maximum(a, b), 0.0)


def twice_flux(left, right, nx, ny):
    n2 = HEAT_RATIO * (nx * nx + ny * ny)

    def one(state):
        rho, u, v, p, q = state
        mu, mv, mq = rho * u, rho * v, rho * q
        energy = (1.0 / (HEAT_RATIO - 1.0)) * p + 0.5 * (mu * u + mv * v)
        speed = u * nx + v * ny
        x = p * n2
        wave = jnp.abs(speed) + x * lax.rsqrt(jnp.maximum(x * rho, 1e-30))
        flux = (rho * speed, mu * speed + p * nx, mv * speed + p * ny, (energy + p) * speed, mq * speed)
        return (rho, mu, mv, energy, mq), flux, wave

    cl, fl, sl = one(left)
    cr, fr, sr = one(right)
    s = jnp.maximum(sl, sr)
    return [fl[k] + fr[k] - s * (cr[k] - cl[k]) for k in range(5)]


def each_row(body, unroll):
    def steps(i, carry):
        for n in range(unroll):
            body(i * unroll + n)
        return carry

    if unroll >= BAND:
        for t in range(BAND):
            body(t)
    else:
        lax.fori_loop(0, BAND // unroll, steps, 0)


def primitives_of(rho, mx, my, en, tr):
    inv = 1.0 / rho
    u, v = mx * inv, my * inv
    p = (HEAT_RATIO - 1.0) * (en - 0.5 * (mx * u + my * v))
    return rho, u, v, p, tr * inv


def wrap_prim(prim):
    for k in range(5):
        prim[k, 0] = prev_band(prim[k, BAND])
        prim[k, 1] = prev_band(prim[k, BAND + 1])
        prim[k, BAND + 2] = next_band(prim[k, 2])
        prim[k, BAND + 3] = next_band(prim[k, 3])


def wrap_rows(ref, *lead):
    ref[(*lead, 0)] = prev_band(ref[(*lead, BAND)])
    ref[(*lead, BAND + 1)] = next_band(ref[(*lead, 1)])


def to_weight(prim, weight):
    def body(t):
        g = 0.0
        for k in (0, 3):
            x = prim[k, t + 2]
            a = next_col(x) - prev_col(x)
            b = prim[k, t + 3] - prim[k, t + 1]
            g = g + (a * a + b * b)
        g = (0.25 * GRADIENT_GAIN) * g
        weight[t + 1] = (1.0 + MONITOR_GAIN) - MONITOR_GAIN / (1.0 + g)

    each_row(body, U_WEIGHT)
    wrap_rows(weight)


def to_coefs(weight, coef):
    def body(t):
        c = weight[t + 1]
        e = c + next_col(c)
        w = c + prev_col(c)
        n = c + weight[t + 2]
        s = c + weight[t]
        k = 0.5 / ((e + w) + (n + s))
        coef[0, t] = e * k
        coef[1, t] = w * k
        coef[2, t] = n * k
        coef[3, t] = s * k

    each_row(body, U_COEF)


def sweep(src, dst, coef):
    def body(t):
        he, hw, hn, hs = coef[0, t], coef[1, t], coef[2, t], coef[3, t]
        for k in range(2):
            x = src[k, t + 1]
            source = he - hw if k == 0 else hn - hs
            beside = he * next_col(x) + hw * prev_col(x) + (hn * src[k, t + 2] + hs * src[k, t])
            dst[k, t + 1] = (0.5 * x + source) + beside

    each_row(body, U_SWEEP)
    for k in range(2):
        wrap_rows(dst, k)


def to_metrics(disp, face, slope):
    def body(t):
        dx, dy = disp[0, t + 1], disp[1, t + 1]
        xc = 1.0 + 0.5 * (next_col(dx) - prev_col(dx))
        yc = 0.5 * (next_col(dy) - prev_col(dy))
        xr = 0.5 * (disp[0, t + 2] - disp[0, t])
        yr = 1.0 + 0.5 * (disp[1, t + 2] - disp[1, t])
        face[0, t] = 0.5 * (yr + next_col(yr))
        face[1, t] = -0.5 * (xr + next_col(xr))
        face[2, t] = (0.5 * TIME_STEP) / (xc * yr - xr * yc)
        slope[0, t] = xc
        slope[1, t] = yc

    each_row(body, U_METRIC)
    for k in range(2):
        slope[k, BAND] = next_band(slope[k, 0])


def to_fluxes(prim, half, side, face, slope, colfl, rowfl):
    def slopes(t):
        for k in range(5):
            x = prim[k, t + 2]
            half[k, t] = minmod(0.5 * (x - prim[k, t + 1]), 0.5 * (prim[k, t + 3] - x))
            d = 0.5 * (next_col(x) - x)
            h = minmod(d, prev_col(d))
            side[k, t] = x + h
            side[5 + k, t] = next_col(x - h)

    each_row(slopes, U_SLOPE)
    for k in range(5):
        half[k, BAND] = next_band(half[k, 0])
    wide = prim.shape[3]

    def fluxes(t):
        for j in range(wide // EDGE):
            at = slice(EDGE * j, EDGE * (j + 1))
            left = [side[k, t, :, at] for k in range(5)]
            right = [side[5 + k, t, :, at] for k in range(5)]
            flux = twice_flux(left, right, face[0, t, :, at], face[1, t, :, at])
            for k in range(5):
                colfl[k, t, :, at] = flux[k]
            nx = -0.5 * (slope[1, t, :, at] + slope[1, t + 1, :, at])
            ny = 0.5 * (slope[0, t, :, at] + slope[0, t + 1, :, at])
            left = [prim[k, t + 2, :, at] + half[k, t, :, at] for k in range(5)]
            right = [prim[k, t + 3, :, at] - half[k, t + 1, :, at] for k in range(5)]
            flux = twice_flux(left, right, nx, ny)
            for k in range(5):
                rowfl[k, t + 1, :, at] = flux[k]

    each_row(fluxes, U_FLUX)
    for k in range(5):
        rowfl[k, 0] = prev_band(rowfl[k, BAND])


def change(k, t, face, colfl, rowfl):
    c = colfl[k, t]
    return face[2, t] * ((c - prev_col(c)) + (rowfl[k, t + 1] - rowfl[k, t]))


def unpack_edges(left, right, k, half):
    lane = lax.broadcasted_iota(jnp.int32, left.shape, 1)
    start = EDGE // 2 * half + SLOT * k
    a = pltpu.roll(right, (EDGE - start) % EDGE, 1)
    b = pltpu.roll(left, (EDGE - SLOT - start) % EDGE, 1)
    return jnp.where(lane < EDGE // 2, a, b)


def join_halos(after, before):
    lane = lax.broadcasted_iota(jnp.int32, after[0].shape, 1)
    low = jnp.where(lane < 32, after[0], pltpu.roll(before[0], EDGE // 2, 1))
    high = jnp.where(lane < 96, pltpu.roll(after[1], EDGE // 2, 1), before[1])
    return jnp.where(lane < EDGE // 2, low, high)


def split_halos(x):
    lane = lax.broadcasted_iota(jnp.int32, x.shape, 1)
    y = pltpu.roll(x, EDGE // 2, 1)
    return jnp.where(lane < EDGE // 2, x, y), jnp.where(lane < EDGE // 2, y, x)


def beside(parts):
    c = lax.axis_index("col")
    return lax.rem(c + parts - 1, parts), lax.rem(c + 1, parts)


def core(u_ref, piece_ref, top_ref, bot_ref, out_ref,
         ext, prim, half, side, face, slope, colfl, rowfl, weight, coef, da, db, cons, flat):
    rows, cols = u_ref.shape[1], u_ref.shape[2]
    tiles = cols // EDGE + 1

    def place(k, row, value):
        for j in range(value.shape[1] // EDGE):
            ext[k, j, row:row + value.shape[0], :] = value[:, EDGE * j:EDGE * (j + 1)]

    before, after = beside(piece_ref.shape[0])
    for k in range(5):
        place(k, PAD, u_ref[k])
        for g in range(HALF // 8):
            left, right = piece_ref[before, DTILES + g], piece_ref[after, DTILES + g]
            for h in range(2):
                row = PAD + HALF * h + 8 * g
                ext[k, tiles - 1, row:row + 8, :] = unpack_edges(left, right, k, h)
    for c in range(piece_ref.shape[0]):
        halos = split_halos(piece_ref[c, DTILES - 1])
        for k in range(2):
            for j in range(tiles - 1):
                ext[5 + k, j, PAD + 8 * c:PAD + 8 * c + 8, :] = piece_ref[c, (tiles - 1) * k + j]
            ext[5 + k, tiles - 1, PAD + 8 * c:PAD + 8 * c + 8, :] = halos[k]
    for k in range(7):
        place(k, 0, top_ref[k])
        place(k, PAD + rows, bot_ref[k])

    def band(k, t):
        return jnp.concatenate([ext[k, j, pl.ds(t, 8, stride=BAND), :] for j in range(tiles)], 1)

    for t in range(BAND):
        for k, x in enumerate(primitives_of(*[band(k, t) for k in range(5)])):
            prim[k, t + 2] = x
    wrap_prim(prim)
    sub = lax.broadcasted_iota(jnp.int32, (8, cols + EDGE), 0)
    for ref, at, hit in ((top_ref, 1, 0), (bot_ref, BAND + 2, 7)):
        outer = [jnp.broadcast_to(ref[4, k:k + 1], (8, cols + EDGE)) for k in range(4)]
        extra = primitives_of(*outer, outer[0])
        for k in (0, 3):
            prim[k, at] = jnp.where(sub == hit, extra[k], prim[k, at])
    for k in range(2):
        for t in range(BAND):
            da[k, t + 1] = band(5 + k, t)
        wrap_rows(da, k)
    to_metrics(da, face, slope)
    to_weight(prim, weight)
    to_coefs(weight, coef)
    src, dst = da, db
    for _ in range(SWEEPS):
        sweep(src, dst, coef)
        src, dst = dst, src
    to_fluxes(prim, half, side, face, slope, colfl, rowfl)
    for t in range(BAND):
        new = [band(k, t) - change(k, t, face, colfl, rowfl) for k in range(5)]
        for k in range(5):
            cons[k, t] = new[k]
        for k, x in enumerate(primitives_of(*new)):
            prim[k, t + 2] = x
    wrap_prim(prim)

    def put(k, t, x):
        for j in range(tiles - 1):
            flat[k, j, pl.ds(t, 8, stride=BAND), :] = x[:, EDGE * j:EDGE * (j + 1)]

    group = lax.axis_index("grp")

    @pl.when(group == 0)
    def _():
        to_metrics(da, face, slope)
        to_fluxes(prim, half, side, face, slope, colfl, rowfl)
        for t in range(BAND):
            for k in range(5):
                put(k, t, cons[k, t] - change(k, t, face, colfl, rowfl))

    @pl.when(group == 1)
    def _():
        for t in range(BAND):
            for k in range(2):
                cons[k, t] = da[k, t + 1]
        to_weight(prim, weight)
        to_coefs(weight, coef)
        src, dst = da, db
        for _ in range(SWEEPS):
            sweep(src, dst, coef)
            src, dst = dst, src
        for t in range(BAND):
            for k in range(2):
                put(k, t, da[k, t + 1])
                put(k + 2, t, (da[k, t + 1] - cons[k, t]) * (1.0 / TIME_STEP))
            put(4, t, weight[t + 1])

    for k in range(5):
        for j in range(tiles - 1):
            out_ref[0, k, :, EDGE * j:EDGE * (j + 1)] = flat[k, j, PAD:PAD + rows, :]


U_WEIGHT = U_COEF = U_SWEEP = U_METRIC = U_SLOPE = 5
U_FLUX = 1


def near(x):
    return pltpu.with_memory_space_constraint(x, pltpu.VMEM)


def compute(u, pieces, top, bot):
    rows, cols = u.shape[1], u.shape[2]
    wide = cols + EDGE
    vec = lambda *lead: pltpu.VMEM((*lead, 8, wide), jnp.float32)
    return pl.pallas_call(
        core,
        out_shape=jax.ShapeDtypeStruct((1, 5, rows, cols), jnp.float32),
        in_specs=[pl.BlockSpec(memory_space=pltpu.VMEM)] * 4,
        out_specs=pl.BlockSpec(memory_space=pltpu.VMEM),
        scratch_shapes=[
            pltpu.VMEM((7, wide // EDGE, EXT, EDGE), jnp.float32),
            vec(5, BAND + 4), vec(5, BAND + 1), vec(10, BAND), vec(3, BAND), vec(2, BAND + 1),
            vec(5, BAND), vec(5, BAND + 1), vec(BAND + 2), vec(4, BAND),
            vec(2, BAND + 2), vec(2, BAND + 2), vec(5, BAND),
            pltpu.VMEM((5, cols // EDGE, EXT, EDGE), jnp.float32),
        ],
        name="euler_mesh",
    )(u, near(pieces), near(top), near(bot))


def pack(first_ref, last_ref, disp_ref, piece_ref):
    parts = piece_ref.shape[0]
    tiles = DTILES // 2
    cols = EDGE * tiles
    before, after = beside(parts)
    lane = lax.broadcasted_iota(jnp.int32, (8, EDGE), 1)
    for g in range(HALF // 8):
        first = last = None
        for half in range(2):
            rows = slice(HALF * half + 8 * g, HALF * half + 8 * g + 8)
            for k in range(5):
                start = EDGE // 2 * half + SLOT * k
                a = pltpu.roll(first_ref[k, rows], start, 1) if start else first_ref[k, rows]
                b = pltpu.roll(last_ref[k, rows], SLOT + start, 1)
                first = a if first is None else jnp.where(lane < start, first, a)
                last = b if last is None else jnp.where(lane < start, last, b)
        piece_ref[before, DTILES + g] = first
        piece_ref[after, DTILES + g] = last
    for c in range(parts):
        right = cols * ((c + 1) % parts)
        left = cols * ((c - 1) % parts) + cols - EDGE
        for k in range(2):
            for j in range(tiles):
                at = cols * c + EDGE * j
                piece_ref[c, tiles * k + j] = disp_ref[k, :, at:at + EDGE]
        piece_ref[c, DTILES - 1] = join_halos(
            [disp_ref[k, :, right:right + EDGE] for k in range(2)],
            [disp_ref[k, :, left:left + EDGE] for k in range(2)],
        )


def rim(top_ref, bot_ref, piece_ref, up_ref, down_ref):
    cols = top_ref.shape[2]
    tiles = cols // EDGE + 1
    end = bot_ref.shape[1] - 8
    parts = piece_ref.shape[0]
    before, after = beside(parts)
    final = DTILES + HALF // 8 - 1
    l0, r0 = piece_ref[before, DTILES], piece_ref[after, DTILES]
    l1, r1 = piece_ref[before, final], piece_ref[after, final]
    l2, r2 = piece_ref[before, DTILES + 1], piece_ref[after, DTILES + 1]
    l3, r3 = piece_ref[before, final - 1], piece_ref[after, final - 1]

    def inner(k):
        up_ref[k, :, :cols] = top_ref[k, :8]
        up_ref[k, :, cols:] = unpack_edges(l0, r0, k, 0)
        down_ref[k, :, :cols] = bot_ref[k, end:]
        down_ref[k, :, cols:] = unpack_edges(l1, r1, k, 1)

    for k in range(4):
        inner(k)
    group = lax.axis_index("grp")

    @pl.when(group == 0)
    def _():
        inner(4)

    @pl.when(group == 1)
    def _():
        for k in range(4):
            up_ref[4, k:k + 1, :cols] = top_ref[k, 8:9]
            up_ref[4, k:k + 1, cols:] = unpack_edges(l2, r2, k, 0)[:1]
            up_ref[4, 4 + k:5 + k, :] = jnp.zeros((1, cols + EDGE), jnp.float32)
            down_ref[4, k:k + 1, :cols] = bot_ref[k, end - 1:end]
            down_ref[4, k:k + 1, cols:] = unpack_edges(l3, r3, k, 1)[7:]
            down_ref[4, 4 + k:5 + k, :] = jnp.zeros((1, cols + EDGE), jnp.float32)

    for ref, c in ((up_ref, 0), (down_ref, parts - 1)):
        halos = split_halos(piece_ref[c, DTILES - 1])
        for k in range(2):
            for j in range(tiles - 1):
                ref[5 + k, :, EDGE * j:EDGE * (j + 1)] = piece_ref[c, (tiles - 1) * k + j]
            ref[5 + k, :, cols:] = halos[k]


def shift(x, axis, step):
    count = lax.axis_size(axis)
    return lax.ppermute(x, axis, [(i, (i + step) % count) for i in range(count)])


def on_device(conserved, displacement):
    rows, cols = conserved.shape[1:]
    parts = lax.axis_size("col")
    f32 = jnp.float32
    at = lambda shape, *index: pl.BlockSpec(shape, lambda i: index)
    whole = pl.BlockSpec(memory_space=pltpu.VMEM)
    pieces = pl.pallas_call(
        pack,
        out_shape=pltpu.VMEM((parts, DTILES + HALF // 8, 8, EDGE), f32),
        grid=(1,),
        in_specs=[
            at((5, rows, EDGE), 0, 0, 0),
            at((5, rows, EDGE), 0, 0, cols // EDGE - 1),
            at(displacement.shape, 0, 0, 0),
        ],
        out_specs=whole,
        name="pack",
    )(conserved, conserved, displacement)
    pieces = lax.all_to_all(pieces, "col", 0, 0, tiled=True)
    payload = pltpu.VMEM((7, 8, cols + EDGE), f32)
    up, down = pl.pallas_call(
        rim,
        out_shape=(payload, payload),
        grid=(1,),
        in_specs=[
            at((5, 16, cols), 0, 0, 0),
            at((5, 16, cols), 0, rows // 16 - 1, 0),
            whole,
        ],
        out_specs=(whole, whole),
        name="rim",
    )(conserved, conserved, near(pieces))
    top = shift(down, "row", 1)
    bot = shift(up, "row", -1)
    return compute(conserved, pieces, top, bot)


def solution(mesh):
    placed = (P(None, "row", "col"), P(None, ("row", "col"), None))
    return jax.shard_map(
        on_device,
        mesh=mesh,
        in_specs=placed,
        out_specs=P("grp", None, "row", "col"),
        check_vma=False,
    )
```
